128 devices in a mesh: video: 32 (over z_hi, x, y), head: 4 (over z_lo, core).
Axes of the slice: x: 4, y: 4, z: 4 (z_hi: 2, z_lo: 2; z = z_hi * 2 + z_lo), core: 2. Of those that a mesh axis runs over, the one named last changes fastest.
Arguments:
- text_queries: bfloat16 [512, 8192], P('video', 'head'), may hold values from -140 to 140
- visual_keys: bfloat16 [16384, 1024], P('video', 'head'), may hold values from -5 to 5
- visual_values: bfloat16 [16384, 1024], P('video', 'head'), may hold values from -6 to 6
- out_grad: bfloat16 [512, 8192], P('video', 'head'), may hold values from -1536 to 1536
- query_frame: int32 [512], replicated, may hold values from 0 to 15
- block_frame: int32 [128], replicated, may hold values from 0 to 16, as said below
- q_weight: bfloat16 [8192, 8192], P('head', 'video'), may hold values from -0.0625 to 0.0625
Outputs:
- query_grad: bfloat16 [512, 8192], P('video', 'head')
- key_grad: bfloat16 [16384, 1024], P('video', 'head')
- value_grad: bfloat16 [16384, 1024], P('video', 'head')
- text_grad: bfloat16 [512, 8192], P('head', 'video')
The draws below stay inside these ranges and needn't reach their ends.
Inputs may be any that keep to these rules, and one draw needn't show every extreme that they name: `block_frame`: on each index of video the first 1 to 4 block slots are live and the rest empty; some index has all 4 live. Live blocks carry frame numbers that never fall along the whole array and start at 0; empty slots carry 16.
All inputs are finite; a program needn't handle non-finite values.
Results may differ from the reference program's by a relative error of at most 0.0058.
Values may be sent and summed in bfloat16 or wider, within the bound.
No kernel may reach another device: no remote copies, remote signals or barrier semaphores. Data moves between devices by JAX's collectives and lax.ppermute only.
A program may use at most 384 MiB of HBM per device.

```python
import jax
import jax.numpy as jnp
from jax import lax

D = 8192
HEADS = 64
KV_HEADS = 8
HEAD_DIM = 128
BLK_DEV = 4
BLOCK = 128
FRAMES = 16
QUERIES = 512
NBLK = 128
NKEYS = 16384


def keys_source(key):
    source = jax.random.normal(jax.random.fold_in(key, 11), (NKEYS, KV_HEADS * HEAD_DIM), jnp.float32)
    source = jnp.clip(source, -5.0, 5.0)
    return source.at[1].set(source[0] * 0.992)


def draw_visual_keys(key, part):
    return keys_source(key).astype(jnp.bfloat16)


def draw_text_queries(key, part):
    drawn = jax.random.normal(jax.random.fold_in(key, 12), (QUERIES, HEADS * HEAD_DIM), jnp.float32)
    drawn = jnp.clip(drawn, -5.0, 5.0)
    return drawn.astype(jnp.bfloat16)


def draw_block_frame(key, part):
    devices = NBLK // BLK_DEV
    counts = jax.random.randint(jax.random.fold_in(key, 21), (devices,), 1, BLK_DEV + 1)
    fullest = jax.random.randint(jax.random.fold_in(key, 22), (), 0, devices)
    counts = jnp.where(jnp.arange(devices) == fullest, BLK_DEV, counts)
    slot_index = jnp.arange(NBLK) % BLK_DEV
    live_slots = (slot_index < jnp.repeat(counts, BLK_DEV)).astype(jnp.int32)
    ranking = jnp.cumsum(live_slots) - 1
    live_total = jnp.sum(live_slots)
    return jnp.where(live_slots > 0, ranking * FRAMES // live_total, FRAMES).astype(jnp.int32)


def set_ends(drawn, stream_key, low, high):
    longest = drawn.shape.index(max(drawn.shape))
    spots = []
    for shift in (0, 1):
        where = [jax.random.randint(jax.random.fold_in(stream_key, axis), (), 0, length) for axis, length in enumerate(drawn.shape)]
        where[longest] = (where[longest] + shift) % drawn.shape[longest]
        spots.append(tuple(where))
    return drawn.at[spots[0]].set(low).at[spots[1]].set(high)


def level_of(stream_key, extent, split, smallest, high):
    gain, own = 1.0, jax.random.fold_in(stream_key, 6)
    for dim, parts in split:
        steps = jnp.exp(jax.random.uniform(jax.random.fold_in(own, dim), (parts,), jnp.float32, smallest / len(split), high / len(split)))
        gain = gain * jnp.repeat(steps, extent[dim] // parts).reshape([-1 if axis == dim else 1 for axis in range(len(extent))])
    return gain


def bell_draw(stream_key, shape, width, most, cuts=(), kind=jnp.bfloat16):
    values = jax.random.normal(stream_key, shape, jnp.float32) * width
    if len(cuts) > 0:
        values = level_of(stream_key, shape, cuts, -0.22, 0.18) * values
    return jnp.clip(values, min=-most, max=most).astype(kind)


def setup_inputs(seed: int = 0) -> dict:
    key_list = jax.random.split(jax.random.key(seed), 8)
    return {
        "text_queries": draw_text_queries(jax.random.fold_in(key_list[7], 71), 0),
        "visual_keys": draw_visual_keys(jax.random.fold_in(key_list[7], 71), 0),
        "visual_values": bell_draw(key_list[2], (NKEYS, KV_HEADS * HEAD_DIM), 1.0, 6.0, ((0, 32), (1, 4))),
        "out_grad": bell_draw(key_list[3], (QUERIES, HEADS * HEAD_DIM), (NKEYS // 64), 1536.0, ((0, 32), (1, 4))),
        "query_frame": set_ends(jax.random.randint(key_list[4], (QUERIES,), 0, FRAMES), jax.random.fold_in(key_list[4], 1), 0, FRAMES - 1).astype(jnp.int32),
        "block_frame": draw_block_frame(jax.random.fold_in(key_list[7], 71), 0),
        "q_weight": bell_draw(key_list[6], (HEADS * HEAD_DIM, D), (HEADS * HEAD_DIM) ** -0.5, 0.0625, ((0, 4), (1, 32))),
    }


neg_fill = -1.0e30


def reference(text_queries, visual_keys, visual_values, out_grad, query_frame, block_frame, q_weight):
    group_size = HEADS // KV_HEADS
    score_scale = HEAD_DIM ** -0.5
    highest = lax.Precision.HIGHEST
    query_heads = text_queries.astype(jnp.float32).reshape(QUERIES, KV_HEADS, group_size, HEAD_DIM)
    grad_heads = out_grad.astype(jnp.float32).reshape(QUERIES, KV_HEADS, group_size, HEAD_DIM)
    key_blocks = visual_keys.astype(jnp.float32).reshape(NBLK, BLOCK, KV_HEADS, HEAD_DIM)
    value_blocks = visual_values.astype(jnp.float32).reshape(NBLK, BLOCK, KV_HEADS, HEAD_DIM)

    def masked(key_block, frame):
        scores = jnp.einsum("rgjd,kgd->rgjk", query_heads, key_block, precision=highest) * score_scale
        visible = (frame <= query_frame)[:, None, None, None]
        return jnp.where(visible, scores, neg_fill), visible

    def forward(running, block_items):
        peaks, totals, weighted = running
        key_block, value_block, frame = block_items
        scores, visible = masked(key_block, frame)
        new_peak = jnp.maximum(peaks, jnp.max(scores, axis=-1))
        rescale = jnp.exp(peaks - new_peak)
        weights = jnp.where(visible, jnp.exp(scores - new_peak[..., None]), 0.0)
        totals = totals * rescale + jnp.sum(weights, axis=-1)
        weighted = weighted * rescale[..., None] + jnp.einsum("rgjk,kgd->rgjd", weights, value_block, precision=highest)
        return (new_peak, totals, weighted), None

    start_state = (jnp.full((QUERIES, KV_HEADS, group_size), neg_fill, jnp.float32),
                   jnp.zeros((QUERIES, KV_HEADS, group_size), jnp.float32),
                   jnp.zeros((QUERIES, KV_HEADS, group_size, HEAD_DIM), jnp.float32))
    final_state, unused = lax.scan(forward, start_state, (key_blocks, value_blocks, block_frame))
    peaks, totals, weighted = final_state
    log_total = peaks + jnp.log(totals)
    row_dots = jnp.sum(grad_heads * (weighted / totals[..., None]), axis=-1)

    def backward(query_sum, block_items):
        key_block, value_block, frame = block_items
        scores, visible = masked(key_block, frame)
        weights = jnp.where(visible, jnp.exp(scores - log_total[..., None]), 0.0)
        value_dots = jnp.einsum("rgjd,kgd->rgjk", grad_heads, value_block, precision=highest)
        grads_half = lax.optimization_barrier((weights * (value_dots - row_dots[..., None])).astype(jnp.bfloat16))
        weight_half = lax.optimization_barrier(weights.astype(jnp.bfloat16))
        score_grads = grads_half.astype(jnp.float32)
        weight_back = weight_half.astype(jnp.float32)
        query_sum = query_sum + jnp.einsum("rgjk,kgd->rgjd", score_grads, key_block, precision=highest) * score_scale
        key_part = jnp.einsum("rgjk,rgjd->kgd", score_grads, query_heads, precision=highest) * score_scale
        value_part = jnp.einsum("rgjk,rgjd->kgd", weight_back, grad_heads, precision=highest)
        return query_sum, (key_part.astype(jnp.bfloat16), value_part.astype(jnp.bfloat16))

    query_start = jnp.zeros((QUERIES, KV_HEADS, group_size, HEAD_DIM), jnp.float32)
    query_sum, key_value = lax.scan(backward, query_start, (key_blocks, value_blocks, block_frame))
    query_grad = query_sum.reshape(QUERIES, HEADS * HEAD_DIM).astype(jnp.bfloat16)
    key_grad = key_value[0].reshape(NKEYS, KV_HEADS * HEAD_DIM)
    value_grad = key_value[1].reshape(NKEYS, KV_HEADS * HEAD_DIM)
    text_grad = jnp.dot(query_grad, q_weight, preferred_element_type=jnp.float32).astype(jnp.bfloat16)
    return (query_grad, key_grad, value_grad, text_grad)
```

```python
import functools
import math

import jax
import jax.numpy as jnp
from jax import lax
from jax.experimental import pallas as pl
from jax.experimental.pallas import tpu as pltpu
from jax.sharding import Mesh
from jax.sharding import PartitionSpec as P

HEADS = 64
KV_HEADS = 8
GROUP = HEADS // KV_HEADS
HEAD_DIM = 128
BLOCK = 128
VIDEO = ("vz", "vx", "vy")
PLANE = ("vx", "vy")
SCALE = HEAD_DIM ** -0.5
SCALE2 = SCALE * math.log2(math.e)
NEG = -1.0e30
CONTRACT_LAST = (((1,), (1,)), ((), ()))


def dot_last(a, b):
    return lax.dot_general(a, b, CONTRACT_LAST, preferred_element_type=jnp.float32)


def dot(a, b):
    return jnp.dot(a, b, preferred_element_type=jnp.float32)


def fold(x):
    return x.reshape(x.shape[0] // 8, 8, x.shape[1])


def forward_kernel(frames, limit, q, do, k0, v0, k1, v1, stats, scores):
    head = pl.program_id(0)
    queries = q[...]
    grads = do[...]
    limits = limit[...]
    half = k0.shape[0] // BLOCK
    top = jnp.full((8, queries.shape[0]), NEG, jnp.float32)
    for b in range(2 * half):
        k, at = (k0, b) if b < half else (k1, b - half)
        bias = jnp.where(frames[b] <= limits, 0.0, NEG)
        s = dot_last(k[at * BLOCK : (at + 1) * BLOCK, :], queries) * SCALE2 + bias
        scores[b] = s
        top = jnp.maximum(top, jnp.max(fold(s), axis=0))
    peak = jnp.max(top, axis=0, keepdims=True)
    total = jnp.zeros((8, queries.shape[0]), jnp.float32)
    dots = jnp.zeros((8, queries.shape[0]), jnp.float32)
    for b in range(2 * half):
        v, at = (v0, b) if b < half else (v1, b - half)
        p = jnp.exp2(scores[b] - peak)
        value_dots = dot_last(v[at * BLOCK : (at + 1) * BLOCK, :], grads)
        total = total + jnp.sum(fold(p), axis=0)
        dots = dots + jnp.sum(fold(p * value_dots), axis=0)
    stats[0, pl.ds(head, 1), :] = peak
    stats[1, pl.ds(head, 1), :] = jnp.sum(total, axis=0, keepdims=True)
    stats[2, pl.ds(head, 1), :] = jnp.sum(dots, axis=0, keepdims=True)


def backward_kernel(
    frames, limit, stats, q, do, k0, v0, k1, v1, dq, dk0, dv0, dk1, dv1, lse, rows, kt, weights, grads_s
):
    head = pl.program_id(0)
    half_keys = k0.shape[0]
    half = half_keys // BLOCK

    @pl.when(head == 0)
    def _():
        parts = stats.shape[0]
        peak = stats[0, 0]
        for i in range(1, parts):
            peak = jnp.maximum(peak, stats[i, 0])
        total = jnp.zeros_like(peak)
        dots = jnp.zeros_like(peak)
        for i in range(parts):
            w = jnp.exp2(stats[i, 0] - peak)
            total = total + w * stats[i, 1]
            dots = dots + w * stats[i, 2]
        lse[...] = peak + jnp.log2(total)
        rows[...] = dots / total

    @pl.when(head % GROUP == 0)
    def _():
        kt[:, :half_keys] = k0[...].T
        kt[:, half_keys:] = k1[...].T

    queries = q[...]
    grads = do[...]
    limits = limit[...]
    log_total = lse[pl.ds(head, 1), :]
    row_dots = rows[pl.ds(head, 1), :]
    for b in range(2 * half):
        k, v, at = (k0, v0, b) if b < half else (k1, v1, b - half)
        bias = jnp.where(frames[b] <= limits, -log_total, NEG)
        s = dot_last(k[at * BLOCK : (at + 1) * BLOCK, :], queries)
        p = jnp.exp2(s * SCALE2 + bias)
        value_dots = dot_last(v[at * BLOCK : (at + 1) * BLOCK, :], grads)
        weights[b * BLOCK : (b + 1) * BLOCK, :] = p.astype(jnp.bfloat16)
        grads_s[b * BLOCK : (b + 1) * BLOCK, :] = (p * (value_dots - row_dots)).astype(jnp.bfloat16)
    dq[...] = dot(kt[...], grads_s[...]).T * SCALE
    for at, dk, dv in ((0, dk0, dv0), (half_keys, dk1, dv1)):
        dk_part = dot(grads_s[at : at + half_keys, :], queries)
        dv_part = dot(weights[at : at + half_keys, :], grads)

        @pl.when(head % GROUP == 0)
        def _():
            dk[...] = dk_part
            dv[...] = dv_part

        @pl.when(head % GROUP != 0)
        def _():
            dk[...] += dk_part
            dv[...] += dv_part


def attention_specs(queries, keys, heads):
    scalar = pl.BlockSpec(memory_space=pltpu.SMEM)
    limit = pl.BlockSpec((1, queries), lambda h: (0, 0))
    q = pl.BlockSpec((queries, HEAD_DIM), lambda h: (0, h))
    do = pl.BlockSpec((queries, HEAD_DIM), lambda h: (0, heads + h))
    kv = pl.BlockSpec((keys, HEAD_DIM), lambda h: (0, h // GROUP))
    return scalar, limit, q, do, kv


def forward_stats(frames, limit, both, k0, v0, k1, v1):
    queries, keys = both.shape[0], k0.shape[0]
    heads = both.shape[1] // (2 * HEAD_DIM)
    scalar, lim, q, do, kv = attention_specs(queries, keys, heads)
    work = heads * queries * 2 * keys
    return pl.pallas_call(
        forward_kernel,
        grid=(heads,),
        in_specs=[scalar, lim, q, do, kv, kv, kv, kv],
        out_specs=pl.BlockSpec((3, heads, queries), lambda h: (0, 0, 0)),
        out_shape=jax.ShapeDtypeStruct((3, heads, queries), jnp.float32),
        scratch_shapes=[pltpu.VMEM((2 * keys // BLOCK, BLOCK, queries), jnp.float32)],
        cost_estimate=pl.CostEstimate(
            flops=4 * work * HEAD_DIM, bytes_accessed=4 * both.size, transcendentals=work
        ),
        name="forward_stats",
    )(frames, limit, both, both, k0, v0, k1, v1)


def backward_grads(frames, limit, stats, both, k0, v0, k1, v1):
    queries, keys = both.shape[0], k0.shape[0]
    heads = both.shape[1] // (2 * HEAD_DIM)
    scalar, lim, q, do, kv = attention_specs(queries, keys, heads)
    work = heads * queries * 2 * keys
    key_out = jax.ShapeDtypeStruct(k0.shape, jnp.float32)
    return pl.pallas_call(
        backward_kernel,
        grid=(heads,),
        in_specs=[scalar, lim, pl.BlockSpec(stats.shape, lambda h: (0, 0, 0, 0)), q, do, kv, kv, kv, kv],
        out_specs=[q, kv, kv, kv, kv],
        out_shape=[jax.ShapeDtypeStruct((queries, heads * HEAD_DIM), jnp.float32)] + [key_out] * 4,
        scratch_shapes=[
            pltpu.VMEM((heads, queries), jnp.float32),
            pltpu.VMEM((heads, queries), jnp.float32),
            pltpu.VMEM((HEAD_DIM, 2 * keys), jnp.bfloat16),
            pltpu.VMEM((2 * keys, queries), jnp.bfloat16),
            pltpu.VMEM((2 * keys, queries), jnp.bfloat16),
        ],
        cost_estimate=pl.CostEstimate(
            flops=10 * work * HEAD_DIM, bytes_accessed=8 * both.size, transcendentals=work
        ),
        name="backward_grads",
    )(frames, limit, stats, both, both, k0, v0, k1, v1)


def gather_copies(x, axes):
    count = lax.axis_size(axes)
    copies = jnp.broadcast_to(x[None], (count,) + x.shape)
    return lax.all_to_all(copies, axes, 0, 0, tiled=True)


def swap_z(x):
    return lax.ppermute(x, "vz", [(0, 1), (1, 0)])


def sum_over_heads(partial):
    me = lax.axis_index("head")
    parts = lax.axis_size("head")
    rows = partial.shape[0] // parts
    total = lax.dynamic_slice_in_dim(partial, me * rows, rows, 0)
    for i in range(1, parts):
        piece = lax.dynamic_slice_in_dim(partial, jnp.bitwise_xor(me, i) * rows, rows, 0)
        total = total + lax.ppermute(piece, "head", [(j, j ^ i) for j in range(parts)])
    return total


def shards(text_queries, visual_keys, visual_values, out_grad, query_frame, block_frame, q_weight):
    z = lax.axis_index("vz")
    plane = lax.axis_index(PLANE)
    side = lax.axis_size(PLANE)
    query_rows = text_queries.shape[0]
    blocks = visual_keys.shape[0] // BLOCK
    other_keys, other_values = swap_z(visual_keys), swap_z(visual_values)
    own_frames = lax.dynamic_slice_in_dim(block_frame, (z * side + plane) * blocks, blocks)
    other_frames = lax.dynamic_slice_in_dim(block_frame, ((1 - z) * side + plane) * blocks, blocks)
    frames = jnp.concatenate([own_frames, other_frames])
    queries = query_rows * side
    limit = lax.dynamic_slice_in_dim(query_frame, z * queries, queries)[None]
    own_both = jnp.concatenate([text_queries, out_grad], axis=1)
    both = gather_copies(own_both, PLANE).reshape(queries, own_both.shape[1])
    keys = (visual_keys, visual_values, other_keys, other_values)
    stats = gather_copies(forward_stats(frames, limit, both, *keys), PLANE)
    dq, dk0, dv0, dk1, dv1 = backward_grads(frames, limit, stats, both, *keys)
    key_grad = ((dk0 + swap_z(dk1)) * SCALE).astype(jnp.bfloat16)
    value_grad = (dv0 + swap_z(dv1)).astype(jnp.bfloat16)
    terms = lax.all_to_all(dq.reshape(side, query_rows, -1), PLANE, 0, 0, tiled=True)
    query_grad = jnp.sum(terms, axis=0).astype(jnp.bfloat16)
    query_all = gather_copies(query_grad, VIDEO).reshape(2 * queries, -1)
    partial_text = jnp.dot(query_all, q_weight, preferred_element_type=jnp.float32)
    text_grad = sum_over_heads(partial_text).astype(jnp.bfloat16)
    return (query_grad, key_grad, value_grad, text_grad)


def solution(mesh):
    split = Mesh(
        mesh.devices.reshape(2, 4, 4, mesh.shape["head"]), ("vz", "vx", "vy", "head")
    )
    placed = (
        P(VIDEO, "head"),
        P(VIDEO, "head"),
        P(VIDEO, "head"),
        P(VIDEO, "head"),
        P(),
        P(),
        P("head", VIDEO),
    )
    return jax.shard_map(
        shards,
        mesh=split,
        in_specs=placed,
        out_specs=(P(VIDEO, "head"), P(VIDEO, "head"), P(VIDEO, "head"), P("head", VIDEO)),
        check_vma=False,
    )
```

```python
import functools
import math

import jax
import jax.numpy as jnp
from jax import lax
from jax.experimental import pallas as pl
from jax.experimental.pallas import tpu as pltpu
from jax.sharding import Mesh
from jax.sharding import PartitionSpec as P

HEADS = 64
KV_HEADS = 8
GROUP = HEADS // KV_HEADS
HEAD_DIM = 128
BLOCK = 128
VIDEO = ("vz", "vx", "vy")
PLANE = ("vx", "vy")
SCALE = HEAD_DIM ** -0.5
SCALE2 = SCALE * math.log2(math.e)
NEG = -1.0e30
CONTRACT_LAST = (((1,), (1,)), ((), ()))


def dot_last(a, b):
    return lax.dot_general(a, b, CONTRACT_LAST, preferred_element_type=jnp.float32)


def dot(a, b):
    return jnp.dot(a, b, preferred_element_type=jnp.float32)


def fold(x):
    return x.reshape(x.shape[0] // 8, 8, x.shape[1])


def forward_kernel(frames, limit, q, do, k0, v0, k1, v1, stats, scores):
    head = pl.program_id(0)
    queries = q[...]
    grads = do[...]
    limits = limit[...]
    half = k0.shape[0] // BLOCK
    top = jnp.full((8, queries.shape[0]), NEG, jnp.float32)
    for b in range(2 * half):
        k, at = (k0, b) if b < half else (k1, b - half)
        bias = jnp.where(frames[b] <= limits, 0.0, NEG)
        s = dot_last(k[at * BLOCK : (at + 1) * BLOCK, :], queries) * SCALE2 + bias
        scores[b] = s
        top = jnp.maximum(top, jnp.max(fold(s), axis=0))
    peak = jnp.max(top, axis=0, keepdims=True)
    total = jnp.zeros((8, queries.shape[0]), jnp.float32)
    dots = jnp.zeros((8, queries.shape[0]), jnp.float32)
    for b in range(2 * half):
        v, at = (v0, b) if b < half else (v1, b - half)
        p = jnp.exp2(scores[b] - peak)
        value_dots = dot_last(v[at * BLOCK : (at + 1) * BLOCK, :], grads)
        total = total + jnp.sum(fold(p), axis=0)
        dots = dots + jnp.sum(fold(p * value_dots), axis=0)
    stats[0, pl.ds(head, 1), :] = peak
    stats[1, pl.ds(head, 1), :] = jnp.sum(total, axis=0, keepdims=True)
    stats[2, pl.ds(head, 1), :] = jnp.sum(dots, axis=0, keepdims=True)


def backward_kernel(
    frames, limit, stats, q, do, k0, v0, k1, v1, dq, dk0, dv0, dk1, dv1, lse, rows, kt, weights, grads_s
):
    head = pl.program_id(0)
    half_keys = k0.shape[0]
    half = half_keys // BLOCK

    @pl.when(head == 0)
    def _():
        parts = stats.shape[0]
        peak = stats[0, 0]
        for i in range(1, parts):
            peak = jnp.maximum(peak, stats[i, 0])
        total = jnp.zeros_like(peak)
        dots = jnp.zeros_like(peak)
        for i in range(parts):
            w = jnp.exp2(stats[i, 0] - peak)
            total = total + w * stats[i, 1]
            dots = dots + w * stats[i, 2]
        lse[...] = peak + jnp.log2(total)
        rows[...] = dots / total

    @pl.when(head % GROUP == 0)
    def _():
        kt[:, :half_keys] = k0[...].T
        kt[:, half_keys:] = k1[...].T

    queries = q[...]
    grads = do[...]
    limits = limit[...]
    log_total = lse[pl.ds(head, 1), :]
    row_dots = rows[pl.ds(head, 1), :]
    for b in range(2 * half):
        k, v, at = (k0, v0, b) if b < half else (k1, v1, b - half)
        bias = jnp.where(frames[b] <= limits, -log_total, NEG)
        s = dot_last(k[at * BLOCK : (at + 1) * BLOCK, :], queries)
        p = jnp.exp2(s * SCALE2 + bias)
        value_dots = dot_last(v[at * BLOCK : (at + 1) * BLOCK, :], grads)
        weights[b * BLOCK : (b + 1) * BLOCK, :] = p.astype(jnp.bfloat16)
        grads_s[b * BLOCK : (b + 1) * BLOCK, :] = (p * (value_dots - row_dots)).astype(jnp.bfloat16)
    dq[...] = dot(kt[...], grads_s[...]).T * SCALE
    for at, dk, dv in ((0, dk0, dv0), (half_keys, dk1, dv1)):
        dk_part = dot(grads_s[at : at + half_keys, :], queries)
        dv_part = dot(weights[at : at + half_keys, :], grads)

        @pl.when(head % GROUP == 0)
        def _():
            dk[...] = dk_part
            dv[...] = dv_part

        @pl.when(head % GROUP != 0)
        def _():
            dk[...] += dk_part
            dv[...] += dv_part


def attention_specs(queries, keys, heads):
    scalar = pl.BlockSpec(memory_space=pltpu.SMEM)
    limit = pl.BlockSpec((1, queries), lambda h: (0, 0))
    q = pl.BlockSpec((queries, HEAD_DIM), lambda h: (0, h))
    do = pl.BlockSpec((queries, HEAD_DIM), lambda h: (0, heads + h))
    kv = pl.BlockSpec((keys, HEAD_DIM), lambda h: (0, h // GROUP))
    return scalar, limit, q, do, kv


def forward_stats(frames, limit, both, k0, v0, k1, v1):
    queries, keys = both.shape[0], k0.shape[0]
    heads = both.shape[1] // (2 * HEAD_DIM)
    scalar, lim, q, do, kv = attention_specs(queries, keys, heads)
    work = heads * queries * 2 * keys
    return pl.pallas_call(
        forward_kernel,
        grid=(heads,),
        in_specs=[scalar, lim, q, do, kv, kv, kv, kv],
        out_specs=pl.BlockSpec((3, heads, queries), lambda h: (0, 0, 0)),
        out_shape=jax.ShapeDtypeStruct((3, heads, queries), jnp.float32),
        scratch_shapes=[pltpu.VMEM((2 * keys // BLOCK, BLOCK, queries), jnp.float32)],
        cost_estimate=pl.CostEstimate(
            flops=4 * work * HEAD_DIM, bytes_accessed=4 * both.size, transcendentals=work
        ),
        name="forward_stats",
    )(frames, limit, both, both, k0, v0, k1, v1)


def backward_grads(frames, limit, stats, both, k0, v0, k1, v1):
    queries, keys = both.shape[0], k0.shape[0]
    heads = both.shape[1] // (2 * HEAD_DIM)
    scalar, lim, q, do, kv = attention_specs(queries, keys, heads)
    work = heads * queries * 2 * keys
    key_out = jax.ShapeDtypeStruct(k0.shape, jnp.float32)
    return pl.pallas_call(
        backward_kernel,
        grid=(heads,),
        in_specs=[scalar, lim, pl.BlockSpec(stats.shape, lambda h: (0, 0, 0, 0)), q, do, kv, kv, kv, kv],
        out_specs=[q, kv, kv, kv, kv],
        out_shape=[jax.ShapeDtypeStruct((queries, heads * HEAD_DIM), jnp.float32)] + [key_out] * 4,
        scratch_shapes=[
            pltpu.VMEM((heads, queries), jnp.float32),
            pltpu.VMEM((heads, queries), jnp.float32),
            pltpu.VMEM((HEAD_DIM, 2 * keys), jnp.bfloat16),
            pltpu.VMEM((2 * keys, queries), jnp.bfloat16),
            pltpu.VMEM((2 * keys, queries), jnp.bfloat16),
        ],
        cost_estimate=pl.CostEstimate(
            flops=10 * work * HEAD_DIM, bytes_accessed=8 * both.size, transcendentals=work
        ),
        name="backward_grads",
    )(frames, limit, stats, both, both, k0, v0, k1, v1)


def gather_copies(x, axes):
    count = lax.axis_size(axes)
    copies = jnp.broadcast_to(x[None], (count,) + x.shape)
    return lax.all_to_all(copies, axes, 0, 0, tiled=True)


def swap_z(x):
    return lax.ppermute(x, "vz", [(0, 1), (1, 0)])


def text_kernel(rows, weight, out):
    out[0] = dot(rows[...], weight[0])


def text_product(rows, weight):
    count, depth, columns = weight.shape
    return pl.pallas_call(
        text_kernel,
        grid=(count,),
        in_specs=[
            pl.BlockSpec(rows.shape, lambda i: (0, 0)),
            pl.BlockSpec((1, depth, columns), lambda i: (i, 0, 0)),
        ],
        out_specs=pl.BlockSpec((1, rows.shape[0], columns), lambda i: (i, 0, 0)),
        out_shape=jax.ShapeDtypeStruct((count, rows.shape[0], columns), jnp.float32),
        cost_estimate=pl.CostEstimate(
            flops=2 * rows.size * count * columns, bytes_accessed=2 * weight.size, transcendentals=0
        ),
        name="text_product",
    )(rows, weight)


def shards(text_queries, visual_keys, visual_values, out_grad, query_frame, block_frame, q_weight):
    z = lax.axis_index("vz")
    plane = lax.axis_index(PLANE)
    side = lax.axis_size(PLANE)
    query_rows = text_queries.shape[0]
    blocks = visual_keys.shape[0] // BLOCK
    other_keys, other_values = swap_z(visual_keys), swap_z(visual_values)
    own_frames = lax.dynamic_slice_in_dim(block_frame, (z * side + plane) * blocks, blocks)
    other_frames = lax.dynamic_slice_in_dim(block_frame, ((1 - z) * side + plane) * blocks, blocks)
    frames = jnp.concatenate([own_frames, other_frames])
    queries = query_rows * side
    limit = lax.dynamic_slice_in_dim(query_frame, z * queries, queries)[None]
    own_both = jnp.concatenate([text_queries, out_grad], axis=1)
    both = gather_copies(own_both, PLANE).reshape(queries, own_both.shape[1])
    both, other_keys, other_values, q_weight = lax.optimization_barrier(
        (both, other_keys, other_values, q_weight)
    )
    keys = (visual_keys, visual_values, other_keys, other_values)
    weight = lax.all_gather(q_weight, "vy")
    stats = gather_copies(forward_stats(frames, limit, both, *keys), PLANE)
    dq, dk0, dv0, dk1, dv1 = backward_grads(frames, limit, stats, both, *keys)
    terms = lax.all_to_all(dq.reshape(side, query_rows, -1), PLANE, 0, 0, tiled=True)
    terms, dk1, dv1 = lax.optimization_barrier((terms, swap_z(dk1), swap_z(dv1)))
    query_grad = jnp.sum(terms, axis=0).astype(jnp.bfloat16)
    key_grad = ((dk0 + dk1) * SCALE).astype(jnp.bfloat16)
    value_grad = (dv0 + dv1).astype(jnp.bfloat16)
    rows = gather_copies(query_grad, ("vz", "vx"))
    text = text_product(rows.reshape(-1, rows.shape[-1]), weight)
    lines, parts = lax.axis_size("vy"), lax.axis_size("head")
    text = text.reshape(lines * parts, text.shape[1] // parts, text.shape[2])
    text = lax.all_to_all(text, ("vy", "head"), 0, 0, tiled=True)
    text = jnp.sum(text.reshape(lines, parts, -1, query_rows, text.shape[2]), axis=1)
    text_grad = text.transpose(1, 0, 2, 3).reshape(-1, text.shape[3]).astype(jnp.bfloat16)
    return (query_grad, key_grad, value_grad, text_grad)


def solution(mesh):
    split = Mesh(
        mesh.devices.reshape(2, 4, 4, mesh.shape["head"]), ("vz", "vx", "vy", "head")
    )
    placed = (
        P(VIDEO, "head"),
        P(VIDEO, "head"),
        P(VIDEO, "head"),
        P(VIDEO, "head"),
        P(),
        P(),
        P("head", VIDEO),
    )
    return jax.shard_map(
        shards,
        mesh=split,
        in_specs=placed,
        out_specs=(P(VIDEO, "head"), P(VIDEO, "head"), P(VIDEO, "head"), P("head", VIDEO)),
        check_vma=False,
    )
```

```python
import functools
import math

import jax
import jax.numpy as jnp
from jax import lax
from jax.experimental import pallas as pl
from jax.experimental.pallas import tpu as pltpu
from jax.sharding import Mesh
from jax.sharding import PartitionSpec as P

HEADS = 64
KV_HEADS = 8
GROUP = HEADS // KV_HEADS
HEAD_DIM = 128
BLOCK = 128
VIDEO = ("vz", "vx", "vy")
PLANE = ("vx", "vy")
SCALE = HEAD_DIM ** -0.5
SCALE2 = SCALE * math.log2(math.e)
NEG = -1.0e30
CONTRACT_LAST = (((1,), (1,)), ((), ()))


def dot_last(a, b):
    return lax.dot_general(a, b, CONTRACT_LAST, preferred_element_type=jnp.float32)


def dot(a, b):
    return jnp.dot(a, b, preferred_element_type=jnp.float32)


def fold(x):
    return x.reshape(x.shape[0] // 8, 8, x.shape[1])


def pieces_of(x):
    high = x.astype(jnp.bfloat16).astype(jnp.float32)
    rest = x - high
    middle = rest.astype(jnp.bfloat16).astype(jnp.float32)
    return [high, middle, rest - middle]


def local_kernel(frames, limit, q, do, k0, v0, k1, v1, sums, stats, scores, dots, weights, grads_s, kt):
    step = pl.program_id(0)
    heads = stats.shape[1]
    half_keys = k0.shape[0]
    half = half_keys // BLOCK

    @pl.when(jnp.logical_and(step % GROUP == 0, step < heads))
    def _():
        kt[:, :half_keys] = k0[...].T
        kt[:, half_keys:] = k1[...].T

    @pl.when(step < heads)
    def _():
        queries = q[...]
        grads = do[...]
        limits = limit[...]
        top = jnp.full((8, queries.shape[0]), NEG, jnp.float32)
        for b in range(2 * half):
            k, at = (k0, b) if b < half else (k1, b - half)
            bias = jnp.where(frames[b] <= limits, 0.0, NEG)
            s = dot_last(k[at * BLOCK : (at + 1) * BLOCK, :], queries) * SCALE2 + bias
            scores[b] = s
            top = jnp.maximum(top, jnp.max(fold(s), axis=0))
        peak = jnp.max(top, axis=0, keepdims=True)
        total = jnp.zeros((8, queries.shape[0]), jnp.float32)
        moment = jnp.zeros((8, queries.shape[0]), jnp.float32)
        for b in range(2 * half):
            v, at = (v0, b) if b < half else (v1, b - half)
            p = jnp.exp2(scores[b] - peak)
            value_dots = dot_last(v[at * BLOCK : (at + 1) * BLOCK, :], grads)
            scores[b] = p
            dots[b] = value_dots
            weights[b * BLOCK : (b + 1) * BLOCK, :] = p.astype(jnp.bfloat16)
            total = total + jnp.sum(fold(p), axis=0)
            moment = moment + jnp.sum(fold(p * value_dots), axis=0)
        total = jnp.sum(total, axis=0, keepdims=True)
        share = 1.0 / total
        mean = jnp.sum(moment, axis=0, keepdims=True) * share
        for b in range(2 * half):
            grads_s[b * BLOCK : (b + 1) * BLOCK, :] = (scores[b] * (dots[b] - mean)).astype(jnp.bfloat16)
        sums[:, :HEAD_DIM] = (dot(kt[...], grads_s[...]) * share).T.astype(jnp.bfloat16)
        sums[:, HEAD_DIM:] = (dot(kt[...], weights[...]) * share).T.astype(jnp.bfloat16)
        stats[0, pl.ds(step, 1), :] = peak + jnp.log2(total)
        stats[1, pl.ds(step, 1), :] = mean

    @pl.when(step == heads)
    def _():
        rows = pieces_of(stats[0]) + pieces_of(stats[1])
        rows = jnp.concatenate(rows + [jnp.zeros_like(rows[0])] * 2, axis=0)
        sums[:, :HEAD_DIM] = rows.T.astype(jnp.bfloat16)
        sums[:, HEAD_DIM:] = jnp.zeros_like(sums[:, HEAD_DIM:])


def keys_kernel(frames, limit, lse, rows, q, do, k0, v0, k1, v1, dk0, dv0, dk1, dv1, weights, grads_s):
    head = pl.program_id(0)
    half_keys = k0.shape[0]
    half = half_keys // BLOCK
    queries = q[...]
    grads = do[...]
    limits = limit[...]
    log_total = lse[pl.ds(head, 1), :]
    row_dots = rows[pl.ds(head, 1), :]
    for b in range(2 * half):
        k, v, at = (k0, v0, b) if b < half else (k1, v1, b - half)
        bias = jnp.where(frames[b] <= limits, -log_total, NEG)
        s = dot_last(k[at * BLOCK : (at + 1) * BLOCK, :], queries)
        p = jnp.exp2(s * SCALE2 + bias)
        value_dots = dot_last(v[at * BLOCK : (at + 1) * BLOCK, :], grads)
        weights[b * BLOCK : (b + 1) * BLOCK, :] = p.astype(jnp.bfloat16)
        grads_s[b * BLOCK : (b + 1) * BLOCK, :] = (p * (value_dots - row_dots)).astype(jnp.bfloat16)
    for at, dk, dv in ((0, dk0, dv0), (half_keys, dk1, dv1)):
        dk_part = dot(grads_s[at : at + half_keys, :], queries)
        dv_part = dot(weights[at : at + half_keys, :], grads)

        @pl.when(head % GROUP == 0)
        def _():
            dk[...] = dk_part
            dv[...] = dv_part

        @pl.when(head % GROUP != 0)
        def _():
            dk[...] += dk_part
            dv[...] += dv_part


def combine_kernel(terms, out):
    sources = terms.shape[0]
    heads = out.shape[2] // HEAD_DIM
    tops, means = [], []
    for i in range(sources):
        t = terms[i, :, 2 * heads * HEAD_DIM : (2 * heads + 1) * HEAD_DIM].astype(jnp.float32)
        t = t + pltpu.roll(t, HEAD_DIM - heads, 1) + pltpu.roll(t, HEAD_DIM - 2 * heads, 1)
        tops.append(t)
        means.append(pltpu.roll(t, HEAD_DIM - 3 * heads, 1))
    peak = functools.reduce(jnp.maximum, tops)
    shares = [jnp.exp2(t - peak) for t in tops]
    total = sum(shares)
    row_dots = sum(w * m for w, m in zip(shares, means)) / total
    scale = SCALE / total
    factors = [w * scale for w in shares]
    shifts = [f * (m - row_dots) for f, m in zip(factors, means)]
    for j in range(heads):
        result = jnp.zeros((terms.shape[1], HEAD_DIM), jnp.float32)
        for part, scales in enumerate((factors, shifts)):
            at = (2 * j + part) * HEAD_DIM
            for i in range(sources):
                result = result + scales[i][:, j : j + 1] * terms[i, :, at : at + HEAD_DIM].astype(jnp.float32)
        for i in range(out.shape[0]):
            out[i, :, j * HEAD_DIM : (j + 1) * HEAD_DIM] = result.astype(jnp.bfloat16)


def attention_specs(queries, keys, heads):
    scalar = pl.BlockSpec(memory_space=pltpu.SMEM)
    limit = pl.BlockSpec((1, queries), lambda h: (0, 0))
    q = pl.BlockSpec((queries, HEAD_DIM), lambda h: (0, h))
    do = pl.BlockSpec((queries, HEAD_DIM), lambda h: (0, heads + h))
    kv = pl.BlockSpec((keys, HEAD_DIM), lambda h: (0, h // GROUP))
    return scalar, limit, q, do, kv


def local_sums(frames, limit, both, k0, v0, k1, v1):
    queries, keys = both.shape[0], k0.shape[0]
    heads = both.shape[1] // (2 * HEAD_DIM)
    last = heads - 1
    scalar = pl.BlockSpec(memory_space=pltpu.SMEM)
    lim = pl.BlockSpec((1, queries), lambda h: (0, 0))
    q = pl.BlockSpec((queries, HEAD_DIM), lambda h: (0, jnp.minimum(h, last)))
    do = pl.BlockSpec((queries, HEAD_DIM), lambda h: (0, heads + jnp.minimum(h, last)))
    kv = pl.BlockSpec((keys, HEAD_DIM), lambda h: (0, jnp.minimum(h, last) // GROUP))
    work = heads * queries * 2 * keys
    blocks = 2 * keys // BLOCK
    return pl.pallas_call(
        local_kernel,
        grid=(heads + 1,),
        in_specs=[scalar, lim, q, do, kv, kv, kv, kv],
        out_specs=[
            pl.BlockSpec((queries, 2 * HEAD_DIM), lambda h: (0, h)),
            pl.BlockSpec((2, heads, queries), lambda h: (0, 0, 0)),
        ],
        out_shape=[
            jax.ShapeDtypeStruct((queries, (heads + 1) * 2 * HEAD_DIM), jnp.bfloat16),
            jax.ShapeDtypeStruct((2, heads, queries), jnp.float32),
        ],
        scratch_shapes=[
            pltpu.VMEM((blocks, BLOCK, queries), jnp.float32),
            pltpu.VMEM((blocks, BLOCK, queries), jnp.float32),
            pltpu.VMEM((2 * keys, queries), jnp.bfloat16),
            pltpu.VMEM((2 * keys, queries), jnp.bfloat16),
            pltpu.VMEM((HEAD_DIM, 2 * keys), jnp.bfloat16),
        ],
        cost_estimate=pl.CostEstimate(
            flops=8 * work * HEAD_DIM, bytes_accessed=8 * both.size, transcendentals=work
        ),
        name="local_sums",
    )(frames, limit, both, both, k0, v0, k1, v1)


def key_value_grads(frames, limit, lse, row_dots, both, k0, v0, k1, v1):
    queries, keys = both.shape[0], k0.shape[0]
    heads = both.shape[1] // (2 * HEAD_DIM)
    scalar, lim, q, do, kv = attention_specs(queries, keys, heads)
    work = heads * queries * 2 * keys
    row = pl.BlockSpec((heads, queries), lambda h: (0, 0))
    return pl.pallas_call(
        keys_kernel,
        grid=(heads,),
        in_specs=[scalar, lim, row, row, q, do, kv, kv, kv, kv],
        out_specs=[kv, kv, kv, kv],
        out_shape=[jax.ShapeDtypeStruct(k0.shape, jnp.float32)] * 4,
        scratch_shapes=[
            pltpu.VMEM((2 * keys, queries), jnp.bfloat16),
            pltpu.VMEM((2 * keys, queries), jnp.bfloat16),
        ],
        cost_estimate=pl.CostEstimate(
            flops=8 * work * HEAD_DIM, bytes_accessed=8 * both.size, transcendentals=work
        ),
        name="key_value_grads",
    )(frames, limit, lse, row_dots, both, both, k0, v0, k1, v1)


def combine_terms(terms, heads, copies):
    vmem = pl.BlockSpec(memory_space=pltpu.VMEM)
    return pl.pallas_call(
        combine_kernel,
        in_specs=[vmem],
        out_specs=vmem,
        out_shape=jax.ShapeDtypeStruct((copies, terms.shape[1], heads * HEAD_DIM), jnp.bfloat16),
        cost_estimate=pl.CostEstimate(
            flops=2 * terms.size, bytes_accessed=2 * terms.size, transcendentals=0
        ),
        name="combine_terms",
    )(terms)


def merge_stats(stats, axis):
    size = lax.axis_size(axis)
    parts = [stats]
    for shift in range(1, size):
        parts.append(lax.ppermute(stats, axis, [(i, (i + shift) % size) for i in range(size)]))
    peak = functools.reduce(jnp.maximum, [p[0] for p in parts])
    shares = [jnp.exp2(p[0] - peak) for p in parts]
    total = sum(shares)
    mean = sum(w * p[1] for w, p in zip(shares, parts)) / total
    return jnp.stack([peak + jnp.log2(total), mean])


def gather_copies(x, axes):
    count = lax.axis_size(axes)
    copies = jnp.broadcast_to(x[None], (count,) + x.shape)
    return lax.all_to_all(copies, axes, 0, 0, tiled=True)


def swap_z(x):
    return lax.ppermute(x, "vz", [(0, 1), (1, 0)])


def line_pieces(x):
    half = x.shape[0] // 2
    ahead = [(i, (i + 1) % 4) for i in range(4)]
    back = [(i, (i + 3) % 4) for i in range(4)]
    below = lax.ppermute(x, "vy", ahead)
    above = lax.ppermute(x, "vy", back)
    return x, below, above, lax.ppermute(below[:half], "vy", ahead), lax.ppermute(above[half:], "vy", back)


def text_kernel(line, rows, own, below, above, far0, far1, out):
    count = out.shape[0]
    half = far0.shape[0]
    me = line[0]
    out[me] = dot(rows[...], own[...])
    out[lax.rem(me + count - 1, count)] = dot(rows[...], below[...])
    out[lax.rem(me + 1, count)] = dot(rows[...], above[...])
    out[lax.rem(me + 2, count)] = dot(rows[:, :half], far0[...]) + dot(rows[:, half:], far1[...])


def text_product(rows, weights):
    count = lax.axis_size("vy")
    depth, columns = weights[0].shape
    vmem = pl.BlockSpec(memory_space=pltpu.VMEM)
    return pl.pallas_call(
        text_kernel,
        in_specs=[pl.BlockSpec(memory_space=pltpu.SMEM)] + [vmem] * 6,
        out_specs=vmem,
        out_shape=jax.ShapeDtypeStruct((count, rows.shape[0], columns), jnp.float32),
        cost_estimate=pl.CostEstimate(
            flops=2 * rows.size * count * columns, bytes_accessed=2 * count * depth * columns, transcendentals=0
        ),
        name="text_product",
    )(lax.axis_index("vy").reshape(1), rows, *weights)


def shards(text_queries, visual_keys, visual_values, out_grad, query_frame, block_frame, q_weight):
    z = lax.axis_index("vz")
    plane = lax.axis_index(PLANE)
    side = lax.axis_size(PLANE)
    query_rows = text_queries.shape[0]
    blocks = visual_keys.shape[0] // BLOCK
    other_keys, other_values = swap_z(visual_keys), swap_z(visual_values)
    own_frames = lax.dynamic_slice_in_dim(block_frame, (z * side + plane) * blocks, blocks)
    other_frames = lax.dynamic_slice_in_dim(block_frame, ((1 - z) * side + plane) * blocks, blocks)
    frames = jnp.concatenate([own_frames, other_frames])
    queries = query_rows * side
    limit = lax.dynamic_slice_in_dim(query_frame, z * queries, queries)[None]
    own_both = jnp.concatenate([text_queries, out_grad], axis=1)
    both = gather_copies(own_both, PLANE).reshape(queries, own_both.shape[1])
    both, other_keys, other_values, q_weight = lax.optimization_barrier(
        (both, other_keys, other_values, q_weight)
    )
    keys = (visual_keys, visual_values, other_keys, other_values)
    sums, stats = local_sums(frames, limit, both, *keys)
    terms = lax.all_to_all(sums.reshape(side, query_rows, -1), PLANE, 0, 0, tiled=True)
    lse, row_dots = merge_stats(merge_stats(stats, "vx"), "vy")
    dk0, dv0, dk1, dv1 = key_value_grads(frames, limit, lse, row_dots, both, *keys)
    copies = combine_terms(terms, text_queries.shape[1] // HEAD_DIM, lax.axis_size(("vz", "vx")))
    rows = lax.all_to_all(copies, ("vz", "vx"), 0, 0, tiled=True)
    query_grad = copies[0]
    key_grad = ((dk0 + swap_z(dk1)) * SCALE).astype(jnp.bfloat16)
    value_grad = (dv0 + swap_z(dv1)).astype(jnp.bfloat16)
    weights = line_pieces(q_weight)
    text = text_product(rows.reshape(-1, rows.shape[-1]), weights)
    lines, parts = lax.axis_size("vy"), lax.axis_size("head")
    text = text.reshape(lines * parts, text.shape[1] // parts, text.shape[2])
    text = lax.all_to_all(text, ("vy", "head"), 0, 0, tiled=True)
    text = jnp.sum(text.reshape(lines, parts, -1, query_rows, text.shape[2]), axis=1)
    text_grad = text.transpose(1, 0, 2, 3).reshape(-1, text.shape[3]).astype(jnp.bfloat16)
    return (query_grad, key_grad, value_grad, text_grad)


def solution(mesh):
    split = Mesh(
        mesh.devices.reshape(2, 4, 4, mesh.shape["head"]), ("vz", "vx", "vy", "head")
    )
    placed = (
        P(VIDEO, "head"),
        P(VIDEO, "head"),
        P(VIDEO, "head"),
        P(VIDEO, "head"),
        P(),
        P(),
        P("head", VIDEO),
    )
    return jax.shard_map(
        shards,
        mesh=split,
        in_specs=placed,
        out_specs=(P(VIDEO, "head"), P(VIDEO, "head"), P(VIDEO, "head"), P("head", VIDEO)),
        check_vma=False,
    )
```

```python
import functools
import math

import jax
import jax.numpy as jnp
from jax import lax
from jax.experimental import pallas as pl
from jax.experimental.pallas import tpu as pltpu
from jax.sharding import Mesh
from jax.sharding import PartitionSpec as P

HEADS = 64
KV_HEADS = 8
GROUP = HEADS // KV_HEADS
HEAD_DIM = 128
BLOCK = 128
VIDEO = ("vz", "vx", "vy")
PLANE = ("vx", "vy")
SCALE = HEAD_DIM ** -0.5
SCALE2 = SCALE * math.log2(math.e)
NEG = -1.0e30
PER_STEP = 4
CONTRACT_LAST = (((1,), (1,)), ((), ()))


def dot_last(a, b):
    return lax.dot_general(a, b, CONTRACT_LAST, preferred_element_type=jnp.float32)


def dot(a, b):
    return jnp.dot(a, b, preferred_element_type=jnp.float32)


def fold(x):
    return x.reshape(x.shape[0] // 8, 8, x.shape[1])


def head_columns(j):
    return slice(j * HEAD_DIM, (j + 1) * HEAD_DIM)


def key_bias(frames, first, limits, seen):
    rows = [jnp.where(frames[first + b] <= limits, seen, NEG) for b in range(frames.shape[0] // 2)]
    return jnp.concatenate([jnp.broadcast_to(r, (BLOCK, r.shape[1])) for r in rows], axis=0)


def forward_kernel(frames, limit, q, do, k0, v0, k1, v1, stats, scores):
    step = pl.program_id(0)
    limits = limit[...]
    half_keys = k0.shape[0]
    half = half_keys // BLOCK
    for j in range(PER_STEP):
        queries = q[:, head_columns(j)]
        grads = do[:, head_columns(j)]
        tops = []
        for at, k in ((0, k0), (1, k1)):
            s = dot_last(k[...], queries) * SCALE2 + key_bias(frames, at * half, limits, 0.0)
            scores[j, at] = s
            tops.append(jnp.max(fold(s), axis=0))
        peak = jnp.max(jnp.maximum(*tops), axis=0, keepdims=True)
        total = jnp.zeros((8, queries.shape[0]), jnp.float32)
        moment = jnp.zeros((8, queries.shape[0]), jnp.float32)
        for at, v in ((0, v0), (1, v1)):
            p = jnp.exp2(scores[j, at] - peak)
            value_dots = dot_last(v[...], grads)
            total = total + jnp.sum(fold(p), axis=0)
            moment = moment + jnp.sum(fold(p * value_dots), axis=0)
        total = jnp.sum(total, axis=0, keepdims=True)
        head = step * PER_STEP + j
        stats[0, pl.ds(head, 1), :] = peak + jnp.log2(total)
        stats[1, pl.ds(head, 1), :] = jnp.sum(moment, axis=0, keepdims=True) / total


def merge_stats(stats):
    sources = stats.shape[0]
    peak = functools.reduce(jnp.maximum, [stats[i, 0] for i in range(sources)])
    shares = [jnp.exp2(stats[i, 0] - peak) for i in range(sources)]
    total = sum(shares)
    row_dots = sum(w * stats[i, 1] for i, w in enumerate(shares)) / total
    return peak + jnp.log2(total), row_dots


def query_kernel(frames, limit, stats, q, do, k0, v0, k1, v1, dq, bias, columns):
    step = pl.program_id(0)
    heads = stats.shape[2]
    half_keys = k0.shape[0]

    @pl.when(step == 0)
    def _():
        limits = limit[...]
        for at in range(2):
            half = half_keys // BLOCK
            bias[:, at * half_keys : (at + 1) * half_keys] = key_bias(frames, at * half, limits, 0.0).T
        log_total, row_dots = merge_stats(stats)
        filler = jnp.zeros((HEAD_DIM - 2 * PER_STEP, log_total.shape[1]), jnp.float32)
        for i in range(heads // PER_STEP):
            rows = slice(i * PER_STEP, (i + 1) * PER_STEP)
            columns[i] = jnp.concatenate([log_total[rows], row_dots[rows], filler], axis=0).T

    for j in range(PER_STEP):
        queries = q[:, head_columns(j)]
        grads = do[:, head_columns(j)]
        log_total = columns[step, :, j : j + 1]
        row_dots = columns[step, :, PER_STEP + j : PER_STEP + j + 1]
        result = jnp.zeros((queries.shape[0], HEAD_DIM), jnp.float32)
        for at, k, v in ((0, k0, v0), (half_keys, k1, v1)):
            s = dot_last(queries, k[...]) * SCALE2 + bias[:, at : at + half_keys]
            p = jnp.exp2(s - log_total)
            value_dots = dot_last(grads, v[...])
            result = result + dot((p * (value_dots - row_dots)).astype(jnp.bfloat16), k[...])
        dq[:, head_columns(j)] = result * SCALE


def keys_kernel(frames, limit, stats, q, do, k0, v0, k1, v1, dk0, dv0, dk1, dv1, lse, rows):
    step = pl.program_id(0)
    limits = limit[...]
    half = k0.shape[0] // BLOCK

    @pl.when(step == 0)
    def _():
        lse[...], rows[...] = merge_stats(stats)

    first = step % (GROUP // PER_STEP) == 0
    for at, k, v, dk, dv in ((0, k0, v0, dk0, dv0), (half, k1, v1, dk1, dv1)):
        dk_part = jnp.zeros(dk.shape, jnp.float32)
        dv_part = jnp.zeros(dv.shape, jnp.float32)
        for j in range(PER_STEP):
            queries = q[:, head_columns(j)]
            grads = do[:, head_columns(j)]
            head = step * PER_STEP + j
            log_total = lse[pl.ds(head, 1), :]
            row_dots = rows[pl.ds(head, 1), :]
            p = jnp.exp2(dot_last(k[...], queries) * SCALE2 + key_bias(frames, at, limits, -log_total))
            value_dots = dot_last(v[...], grads)
            dk_part = dk_part + dot((p * (value_dots - row_dots)).astype(jnp.bfloat16), queries)
            dv_part = dv_part + dot(p.astype(jnp.bfloat16), grads)

        @pl.when(first)
        def _():
            dk[...] = dk_part
            dv[...] = dv_part

        @pl.when(jnp.logical_not(first))
        def _():
            dk[...] += dk_part
            dv[...] += dv_part


def attention_call(kernel, name, products, frames, limit, stats, both, keys, out_specs, out_shape, scratch):
    queries, key_rows = both.shape[0], keys[0].shape[0]
    steps = both.shape[1] // (2 * HEAD_DIM * PER_STEP)
    work = steps * PER_STEP * queries * 2 * key_rows
    whole = [pl.BlockSpec(x.shape, lambda i, n=x.ndim: (0,) * n) for x in (limit,) + stats]
    q = pl.BlockSpec((queries, PER_STEP * HEAD_DIM), lambda i: (0, i))
    do = pl.BlockSpec((queries, PER_STEP * HEAD_DIM), lambda i: (0, steps + i))
    kv = pl.BlockSpec((key_rows, HEAD_DIM), lambda i: (0, i // (GROUP // PER_STEP)))
    return pl.pallas_call(
        kernel,
        grid=(steps,),
        in_specs=[pl.BlockSpec(memory_space=pltpu.SMEM)] + whole + [q, do, kv, kv, kv, kv],
        out_specs=out_specs(q, kv),
        out_shape=out_shape,
        scratch_shapes=scratch,
        cost_estimate=pl.CostEstimate(
            flops=2 * products * work * HEAD_DIM, bytes_accessed=4 * both.size, transcendentals=work
        ),
        name=name,
    )(frames, limit, *stats, both, both, *keys)


def forward_stats(frames, limit, both, keys):
    queries, key_rows = both.shape[0], keys[0].shape[0]
    shape = (2, both.shape[1] // (2 * HEAD_DIM), queries)
    return attention_call(
        forward_kernel, "forward_stats", 2, frames, limit, (), both, keys,
        lambda q, kv: pl.BlockSpec(shape, lambda i: (0, 0, 0)),
        jax.ShapeDtypeStruct(shape, jnp.float32),
        [pltpu.VMEM((PER_STEP, 2, key_rows, queries), jnp.float32)],
    )


def query_sums(frames, limit, stats, both, keys):
    queries, key_rows = both.shape[0], keys[0].shape[0]
    heads = stats.shape[2]
    return attention_call(
        query_kernel, "query_sums", 3, frames, limit, (stats,), both, keys,
        lambda q, kv: q,
        jax.ShapeDtypeStruct((queries, heads * HEAD_DIM), jnp.float32),
        [
            pltpu.VMEM((queries, 2 * key_rows), jnp.float32),
            pltpu.VMEM((heads // PER_STEP, queries, HEAD_DIM), jnp.float32),
        ],
    )


def key_value_sums(frames, limit, stats, both, keys):
    row = pltpu.VMEM(stats.shape[2:], jnp.float32)
    return attention_call(
        keys_kernel, "key_value_sums", 4, frames, limit, (stats,), both, keys,
        lambda q, kv: [kv] * 4,
        [jax.ShapeDtypeStruct(keys[0].shape, jnp.float32)] * 4,
        [row, row],
    )


def gather_copies(x, axes):
    count = lax.axis_size(axes)
    copies = jnp.broadcast_to(x[None], (count,) + x.shape)
    return lax.all_to_all(copies, axes, 0, 0, tiled=True)


def swap_z(x):
    return lax.ppermute(x, "vz", [(0, 1), (1, 0)])


def line_shift(x, shift):
    count = lax.axis_size("vy")
    return lax.ppermute(x, "vy", [(i, (i + shift) % count) for i in range(count)])


def text_kernel(line, rows, own, below0, below1, above0, above1, far0, far1, out):
    count = out.shape[0]
    half = far0.shape[0]
    me = line[0]
    first, second = rows[:, :half], rows[:, half:]
    out[me] = dot(first, own[:half]) + dot(second, own[half:])
    out[lax.rem(me + count - 1, count)] = dot(first, below0[...]) + dot(second, below1[...])
    out[lax.rem(me + 1, count)] = dot(first, above0[...]) + dot(second, above1[...])
    out[lax.rem(me + 2, count)] = dot(first, far0[...]) + dot(second, far1[...])


def text_product(rows, weights):
    count = lax.axis_size("vy")
    depth, columns = weights[0].shape
    vmem = pl.BlockSpec(memory_space=pltpu.VMEM)
    return pl.pallas_call(
        text_kernel,
        in_specs=[pl.BlockSpec(memory_space=pltpu.SMEM)] + [vmem] * 8,
        out_specs=vmem,
        out_shape=jax.ShapeDtypeStruct((count, rows.shape[0], columns), jnp.float32),
        cost_estimate=pl.CostEstimate(
            flops=2 * rows.size * count * columns, bytes_accessed=2 * count * depth * columns, transcendentals=0
        ),
        name="text_product",
    )(lax.axis_index("vy").reshape(1), rows, *weights)


def shards(text_queries, visual_keys, visual_values, out_grad, query_frame, block_frame, q_weight):
    z = lax.axis_index("vz")
    plane = lax.axis_index(PLANE)
    side = lax.axis_size(PLANE)
    query_rows = text_queries.shape[0]
    blocks = visual_keys.shape[0] // BLOCK
    other_keys, other_values = swap_z(visual_keys), swap_z(visual_values)
    own_frames = lax.dynamic_slice_in_dim(block_frame, (z * side + plane) * blocks, blocks)
    other_frames = lax.dynamic_slice_in_dim(block_frame, ((1 - z) * side + plane) * blocks, blocks)
    frames = jnp.concatenate([own_frames, other_frames])
    queries = query_rows * side
    limit = lax.dynamic_slice_in_dim(query_frame, z * queries, queries)[None]
    own_both = jnp.concatenate([text_queries, out_grad], axis=1)
    both = gather_copies(own_both, PLANE).reshape(queries, own_both.shape[1])
    both, other_keys, other_values, q_weight = lax.optimization_barrier(
        (both, other_keys, other_values, q_weight)
    )
    keys = (visual_keys, visual_values, other_keys, other_values)
    depth = q_weight.shape[0] // 2
    below0, above0 = line_shift(q_weight[:depth], 1), line_shift(q_weight[:depth], -1)
    stats, below0, above0 = lax.optimization_barrier(
        (forward_stats(frames, limit, both, keys), below0, above0)
    )
    stats, later = lax.optimization_barrier((gather_copies(stats, PLANE), q_weight[depth:]))
    below1, above1 = line_shift(later, 1), line_shift(later, -1)
    dq, below0, below1, above1 = lax.optimization_barrier(
        (query_sums(frames, limit, stats, both, keys), below0, below1, above1)
    )
    terms = lax.all_to_all(dq.reshape(side, query_rows, -1), PLANE, 0, 0, tiled=True)
    dk0, dv0, dk1, dv1 = key_value_sums(frames, limit, stats, both, keys)
    query_grad = jnp.sum(terms, axis=0).astype(jnp.bfloat16)
    rows = gather_copies(query_grad, ("vz", "vx"))
    key_grad = ((dk0 + swap_z(dk1)) * SCALE).astype(jnp.bfloat16)
    value_grad = (dv0 + swap_z(dv1)).astype(jnp.bfloat16)
    far0, far1 = line_shift(below0, 1), line_shift(above1, -1)
    weights = (q_weight, below0, below1, above0, above1, far0, far1)
    text = text_product(rows.reshape(-1, rows.shape[-1]), weights)
    lines, parts = lax.axis_size("vy"), lax.axis_size("head")
    text = text.reshape(lines * parts, text.shape[1] // parts, text.shape[2])
    text = lax.all_to_all(text, ("vy", "head"), 0, 0, tiled=True)
    text = jnp.sum(text.reshape(lines, parts, -1, query_rows, text.shape[2]), axis=1)
    text_grad = text.transpose(1, 0, 2, 3).reshape(-1, text.shape[3]).astype(jnp.bfloat16)
    return (query_grad, key_grad, value_grad, text_grad)


def solution(mesh):
    split = Mesh(
        mesh.devices.reshape(2, 4, 4, mesh.shape["head"]), ("vz", "vx", "vy", "head")
    )
    placed = (
        P(VIDEO, "head"),
        P(VIDEO, "head"),
        P(VIDEO, "head"),
        P(VIDEO, "head"),
        P(),
        P(),
        P("head", VIDEO),
    )
    return jax.shard_map(
        shards,
        mesh=split,
        in_specs=placed,
        out_specs=(P(VIDEO, "head"), P(VIDEO, "head"), P(VIDEO, "head"), P("head", VIDEO)),
        check_vma=False,
    )
```
